128 devices in a mesh: shift: 4 (over z), leaf: 32 (over x, y, core).
Axes of the slice: x: 4, y: 4, z: 4, core: 2. Of those that a mesh axis runs over, the one named last changes fastest.
Arguments:
- leaf_rhs: bfloat16 [32, 1024, 1024], P('leaf'), may hold values from -6 to 6
- leaf_inverse: bfloat16 [4, 32, 1024, 1024], P('shift', 'leaf')
- leaf_coupling: bfloat16 [4, 32, 1024, 384], P('shift', 'leaf'), may hold values from -0.1875 to 0.1875
- leaf_rows: int32 [32, 384], P('leaf'), may hold values from 0 to 767, as said below
- front_sizes: int32 [5], replicated, may hold values from 384 to 768, as said below
- front_inverse: bfloat16 [4, 5, 32, 768, 768], P('shift', None, 'leaf'), as said below
- front_coupling: bfloat16 [4, 4, 32, 768, 768], P('shift', None, 'leaf'), as said below
- shift_weight: float32 [4], P('shift'), may hold values from -1 to 1
Outputs:
- filtered: float32 [32, 1024, 1024], P('leaf', 'shift')
The draws below stay inside these ranges and needn't reach their ends.
Inputs may be any that keep to these rules, and one draw needn't show every extreme that they name: `leaf_rows`: the 384 entries of one leaf are distinct. `front_sizes`: the front of at least one level is full. `front_inverse`: all leaves below one separator hold the same front inverse for it. `front_coupling`: all leaves below one separator hold the same coupling for it.
All inputs are finite; a program needn't handle non-finite values.
Results may differ from the reference program's by a relative error of at most 0.01.
Values may be sent and summed in bfloat16 or wider, within the bound.
A program may use at most 128 MiB of HBM per device.

```python
import math
import jax
import jax.numpy as jnp
from jax import lax

L = 1024
FRONT = 768
COLS = 1024
BND = 384
LEAVES = 32
SHIFTS = 4
LEVELS = 5


def rough_noise(key, array_shape):
    return jax.random.normal(key, array_shape, jnp.float32)


def draw_leaf_inverse(key, part):
    diagonal = jax.random.uniform(jax.random.fold_in(key, 11), (SHIFTS, LEAVES, L), jnp.float32, 0.5, 1.5)
    noise = rough_noise(jax.random.fold_in(key, 12), (SHIFTS, LEAVES, L, L)) * (0.5 / math.sqrt(L))
    return (noise + diagonal[..., None] * jnp.eye(L, dtype=jnp.float32)).astype(jnp.bfloat16)


def draw_front_inverse(key, part):
    stacked = []
    for level_index in range(LEVELS):
        stride = 2 ** (level_index + 1)
        node_count = LEAVES // stride
        level_key = jax.random.fold_in(key, 100 + level_index)
        diagonal = jax.random.uniform(jax.random.fold_in(level_key, 1), (SHIFTS, node_count, FRONT), jnp.float32, 0.4, 1.0)
        noise = rough_noise(jax.random.fold_in(level_key, 2), (SHIFTS, node_count, FRONT, FRONT)) * (0.3 / math.sqrt(FRONT))
        block = (noise + diagonal[..., None] * jnp.eye(FRONT, dtype=jnp.float32)).astype(jnp.bfloat16)
        stacked.append(jnp.repeat(block, stride, axis=1))
    return jnp.stack(stacked, axis=1)


def draw_front_coupling(key, part):
    stacked = []
    for level_index in range(LEVELS - 1):
        stride = 2 ** (level_index + 1)
        node_count = LEAVES // stride
        level_key = jax.random.fold_in(key, 200 + level_index)
        block = (rough_noise(level_key, (SHIFTS, node_count, FRONT, FRONT)) / math.sqrt(FRONT)).astype(jnp.bfloat16)
        stacked.append(jnp.repeat(block, stride, axis=1))
    return jnp.stack(stacked, axis=1)


def draw_leaf_rows(key, part):
    scores = jax.random.randint(jax.random.fold_in(key, 31), (LEAVES, FRONT), 0, 2 ** 20) * FRONT
    scores = scores + jnp.arange(FRONT, dtype=jnp.int32)[None, :]
    scores = scores.at[0, 0].set(-2).at[0, FRONT - 1].set(-1)
    ordering = jnp.argsort(scores, axis=1, stable=True)
    return ordering[:, :BND].astype(jnp.int32)


def draw_front_sizes(key, part):
    sizes = jax.random.randint(jax.random.fold_in(key, 41), (LEVELS,), FRONT // 2, FRONT + 1)
    chosen = jax.random.randint(jax.random.fold_in(key, 42), (), 0, LEVELS)
    return jnp.where(jnp.arange(LEVELS) == chosen, FRONT, sizes).astype(jnp.int32)


def shard_levels(own_key, shape, cuts, smallest, largest):
    level, own = 1.0, jax.random.fold_in(own_key, 6)
    for axis_at, blocks in cuts:
        steps = jnp.exp(jax.random.uniform(jax.random.fold_in(own, axis_at), (blocks,), jnp.float32, smallest / len(cuts), largest / len(cuts)))
        level = level * jnp.repeat(steps, shape[axis_at] // blocks).reshape([-1 if axis == axis_at else 1 for axis in range(len(shape))])
    return level


def bell_draw(key, shape, scale, reach, cuts=(), kind=jnp.bfloat16):
    drawn = scale * jax.random.normal(key, shape, jnp.float32)
    if cuts:
        drawn = drawn * shard_levels(key, shape, cuts, -0.22, 0.18)
    return jnp.clip(drawn, -reach, reach).astype(kind)


def setup_inputs(seed: int = 0) -> dict:
    streams_of = jax.random.split(jax.random.key(seed), 9)
    return {
        "leaf_rhs": bell_draw(streams_of[0], (LEAVES, L, COLS), 1.0, 6.0, ((0, 32),)),
        "leaf_inverse": draw_leaf_inverse(jax.random.fold_in(streams_of[8], 71), 0),
        "leaf_coupling": bell_draw(streams_of[2], (SHIFTS, LEAVES, L, BND), L ** -0.5, 0.1875, ((0, 4), (1, 32))),
        "leaf_rows": draw_leaf_rows(jax.random.fold_in(streams_of[8], 71), 0),
        "front_sizes": draw_front_sizes(jax.random.fold_in(streams_of[8], 71), 0),
        "front_inverse": draw_front_inverse(jax.random.fold_in(streams_of[8], 71), 0),
        "front_coupling": draw_front_coupling(jax.random.fold_in(streams_of[8], 71), 0),
        "shift_weight": jnp.clip(jax.random.uniform(streams_of[7], (SHIFTS,), jnp.float32, -1.0, 1.0) * shard_levels(streams_of[7], (SHIFTS,), ((0, 4),), -0.4, 0.0), -1.0, 1.0),
    }


def reference(leaf_rhs, leaf_inverse, leaf_coupling, leaf_rows, front_sizes, front_inverse, front_coupling, shift_weight):
    front_index = jnp.arange(FRONT, dtype=jnp.int32)[:, None]
    accumulated = jnp.zeros((LEAVES, L, COLS), jnp.float32)
    for shift_index in range(SHIFTS):
        def leaf_up(leaf_index):
            leaf_half = jnp.dot(leaf_inverse[shift_index, leaf_index], leaf_rhs[leaf_index], preferred_element_type=jnp.float32).astype(jnp.bfloat16)
            boundary = jnp.dot(leaf_coupling[shift_index, leaf_index].T, leaf_half, preferred_element_type=jnp.float32)
            placed = jnp.zeros((FRONT, COLS), jnp.float32).at[leaf_rows[leaf_index]].add(boundary)
            return leaf_half, placed

        leaf_halves, placed_all = lax.map(leaf_up, jnp.arange(LEAVES, dtype=jnp.int32))
        gathered = placed_all.reshape(LEAVES // 2, 2, FRONT, COLS).sum(axis=1)
        solved_list = []
        mask_list = []
        for level_index in range(LEVELS):
            stride = 2 ** (level_index + 1)
            live_rows = front_index < front_sizes[level_index]
            inverse = front_inverse[shift_index, level_index, ::stride].astype(jnp.float32)
            operand = jnp.where(live_rows, gathered, 0.0).astype(jnp.bfloat16)
            operand = lax.optimization_barrier(operand).astype(jnp.float32)
            solved = jnp.where(live_rows, jnp.einsum('nij,njc->nic', inverse, operand), 0.0).astype(jnp.bfloat16)
            solved_list.append(solved)
            mask_list.append(live_rows)
            if level_index < LEVELS - 1:
                coupling = front_coupling[shift_index, level_index, ::stride].astype(jnp.float32)
                raised = jnp.einsum('nij,nic->njc', coupling, solved.astype(jnp.float32))
                gathered = raised.reshape(raised.shape[0] // 2, 2, FRONT, COLS).sum(axis=1)
        current = solved_list[-1]
        for level_index in range(LEVELS - 2, -1, -1):
            stride = 2 ** (level_index + 1)
            inverse = front_inverse[shift_index, level_index, ::stride].astype(jnp.float32)
            coupling = front_coupling[shift_index, level_index, ::stride].astype(jnp.float32)
            parent = jnp.repeat(current, 2, axis=0).astype(jnp.float32)
            lifted = jnp.einsum('nij,njc->nic', coupling, parent).astype(jnp.bfloat16)
            lifted = lax.optimization_barrier(lifted).astype(jnp.float32)
            correction = jnp.einsum('nij,njc->nic', inverse, lifted)
            current = jnp.where(mask_list[level_index], solved_list[level_index].astype(jnp.float32) - correction, 0.0).astype(jnp.bfloat16)
        parents = jnp.repeat(current, 2, axis=0)

        def leaf_down(leaf_index):
            picked = parents[leaf_index][leaf_rows[leaf_index]]
            lifted = jnp.dot(leaf_coupling[shift_index, leaf_index], picked, preferred_element_type=jnp.float32).astype(jnp.bfloat16)
            solution = leaf_halves[leaf_index].astype(jnp.float32) - jnp.dot(leaf_inverse[shift_index, leaf_index], lifted, preferred_element_type=jnp.float32)
            return shift_weight[shift_index] * solution

        accumulated = accumulated + lax.map(leaf_down, jnp.arange(LEAVES, dtype=jnp.int32))
    return accumulated
```

```python
import jax
import jax.numpy as jnp
from jax import lax
from jax.experimental import pallas as pl
from jax.experimental.pallas import tpu as pltpu
from jax.sharding import PartitionSpec as P

F32 = jnp.float32
BF16 = jnp.bfloat16
NN = (((1,), (0,)), ((), ()))
NT = (((1,), (1,)), ((), ()))
TN = (((0,), (0,)), ((), ()))
STREAMS = 2


def mm(left, right, dims):
    return lax.dot_general(left, right, dims, preferred_element_type=F32)


def kernel(
    rhs_hbm,
    ainv_hbm,
    cpl_hbm,
    rows_ref,
    sizes_ref,
    finv_hbm,
    fcpl_hbm,
    weight_ref,
    out_ref,
    rhs,
    ainv,
    cpl,
    finv,
    fcpl,
    select_t,
    reduced,
    half,
    lift,
    pick_op,
    own0,
    send0,
    recv0,
    solved1,
    solved1_other,
    base,
    own1,
    send1,
    recv1,
    solved2,
    own2,
    send2,
    recv2,
    solved3,
    own3,
    send3,
    recv3,
    solved4,
    own4,
    send4,
    recv4,
    back3,
    back3_other,
    back2,
    back2_other,
    zown,
    zsend1,
    zrecv1,
    zsend2,
    zrecv2,
    load_sem,
    send_sem,
    recv_sem,
):
    leaf_order, _ = ainv.shape
    front = finv.shape[-1]
    bound = cpl.shape[-1]
    wide = rhs.shape[-1] // (4 * STREAMS)
    w = wide // 2
    zrows = out_ref.shape[1]

    p = lax.axis_index("leaf")
    z = lax.axis_index("shift")
    nz = 4
    c = lax.rem(p, 2)
    y = lax.rem(p // 2, 4)
    x = p // 8
    h2 = y // 2
    h1 = lax.rem(lax.rem(y, 2) + h2, 2)

    def leaf_of(xx, yy, cc):
        return {"leaf": (xx * 4 + yy) * 2 + cc}

    core_id = leaf_of(x, y, 1 - c)
    y1_id = leaf_of(x, y + 1 - 2 * lax.rem(y, 2), c)
    y3_id = leaf_of(x, 3 - y, c)
    x1_id = leaf_of(x + 1 - 2 * lax.rem(x, 2), y, c)
    x3_id = leaf_of(3 - x, y, c)
    zp_id = {"shift": lax.rem(z + 1, nz)}
    zm_id = {"shift": lax.rem(z + nz - 1, nz)}
    halves = ((1 - h1, 1 - h2), (1 - h1, h2), (h1, 1 - h2), (h1, h2))

    def column(s, q):
        a, b = halves[q]
        return pl.multiple_of(((a * 2 + b) * STREAMS + s) * wide, wide)

    loads = {}

    def load(name, src, dst):
        copy = pltpu.make_async_copy(src, dst, load_sem.at[len(loads)])
        loads[name] = copy
        copy.start()

    load("cpl", cpl_hbm.at[0, 0], cpl)
    load("ainv", ainv_hbm.at[0, 0], ainv)
    for s in range(STREAMS):
        for q in range(4):
            load(
                ("rhs", s, q),
                rhs_hbm.at[0, :, pl.ds(column(s, q), wide)],
                rhs.at[:, pl.ds((s * 4 + q) * wide, wide)],
            )
    for level in range(5):
        load(("finv", level), finv_hbm.at[0, level, 0], finv.at[level])
        if level < 4:
            load(("fcpl", level), fcpl_hbm.at[0, level, 0], fcpl.at[level])

    barrier = pltpu.get_barrier_semaphore()
    partners = (core_id, y1_id, y3_id, x1_id, x3_id, zp_id, zm_id)
    for partner in partners:
        pl.semaphore_signal(
            barrier, inc=1, device_id=partner, device_id_type=pl.DeviceIdType.MESH
        )
    pl.semaphore_wait(barrier, len(partners))

    sent = {}

    def send(name, src, dst, device):
        copy = pltpu.make_async_remote_copy(
            src_ref=src,
            dst_ref=dst,
            send_sem=send_sem.at[len(sent)],
            recv_sem=recv_sem.at[len(sent)],
            device_id=device,
            device_id_type=pl.DeviceIdType.MESH,
        )
        sent[name] = copy
        copy.start()

    def live(value, level):
        lane = lax.broadcasted_iota(jnp.int32, value.shape, len(value.shape) - 1)
        return jnp.where(lane < sizes_ref[level], value, 0.0)

    tiles = range(0, front, 256)

    def solve(operand, level, dst):
        for n in tiles:
            got = mm(operand, finv[level, n : n + 256, :], NT)
            lane = n + lax.broadcasted_iota(jnp.int32, got.shape, 1)
            dst[:, n : n + 256] = jnp.where(lane < sizes_ref[level], got, 0.0).astype(BF16)

    def raise_to(solved, level, keep, out):
        for n in tiles:
            got = mm(solved, fcpl[level, :, n : n + 256], NN)
            if keep is not None:
                keep[:, n : n + 256] = got
            if out is not None:
                out[:, n : n + 256] = got.astype(BF16)

    def descend(parent, level, solved, dst):
        lifted = jnp.concatenate(
            [mm(parent, fcpl[level, n : n + 256, :], NT).astype(BF16) for n in tiles], axis=1
        )
        for n in tiles:
            got = solved[:, n : n + 256].astype(F32) - mm(
                lifted, finv[level, n : n + 256, :], NT
            )
            lane = n + lax.broadcasted_iota(jnp.int32, got.shape, 1)
            dst[:, n : n + 256] = jnp.where(lane < sizes_ref[level], got, 0.0).astype(BF16)

    for n in range(0, front, 256):
        row = n + lax.broadcasted_iota(jnp.int32, (256, bound), 0)
        select_t[n : n + 256, :] = jnp.where(row == rows_ref[...], 1.0, 0.0).astype(BF16)

    loads["cpl"].wait()
    loads["ainv"].wait()
    for n in range(0, leaf_order, 256):
        reduced[:, n : n + 256] = mm(cpl[...], ainv[:, n : n + 256], TN).astype(BF16)

    for s in range(STREAMS):
        for q in range(4):
            loads["rhs", s, q].wait()
            start = (s * 4 + q) * wide
            boundary = mm(reduced[...], rhs[:, start : start + wide], NN)
            boundary_t = jnp.transpose(boundary).astype(BF16)
            for n in tiles:
                placed = mm(boundary_t, select_t[n : n + 256, :], NT)
                low, high = placed[:w], placed[w:]
                own0[s, q * w : q * w + w, n : n + 256] = jnp.where(c == 0, low, high)
                send0[s, q * w : q * w + w, n : n + 256] = jnp.where(c == 0, high, low).astype(
                    BF16
                )
            if q % 2:
                pair = pl.ds((q - 1) * w, 2 * w)
                send(("place", s, q // 2), send0.at[s, pair], recv0.at[s, pair], core_id)

    loads["finv", 0].wait()
    loads["fcpl", 0].wait()
    for pair in range(2):
        for s in range(STREAMS):
            sent["place", s, pair].wait_recv()
            at = slice(pair * 2 * w, (pair + 1) * 2 * w)
            gathered = own0[s, at, :] + recv0[s, at, :].astype(F32)
            operand = live(gathered, 0).astype(BF16)
            place = pl.ds(s * 4 * w + pair * 2 * w, 2 * w)
            solve(operand, 0, solved1.at[place])
            level1 = solved1[s * 4 * w + pair * 2 * w : s * 4 * w + (pair + 1) * 2 * w, :]
            if pair == 0:
                raise_to(level1, 0, None, send1.at[s])
                for q in range(2):
                    at = pl.ds(q * w, w)
                    send(("up1", s, q), send1.at[s, at], recv1.at[s, at], y1_id)
            else:
                raise_to(level1, 0, own1.at[s], None)
    send("solved1", solved1, solved1_other, core_id)

    for n in range(0, leaf_order, 256):
        half[:, n : n + 256] = mm(ainv[...], rhs[:, n : n + 256], NN).astype(BF16)

    for level in range(1, 5):
        loads["finv", level].wait()
        if level < 4:
            loads["fcpl", level].wait()

    for s in range(STREAMS):
        for q in range(2):
            sent["up1", s, q].wait_recv()
            at = slice(q * w, q * w + w)
            operand = live(own1[s, at, :] + recv1[s, at, :].astype(F32), 1).astype(BF16)
            solve(operand, 1, solved2.at[s, pl.ds(q * w, w)])
            level2 = solved2[s, at, :]
            if q == 0:
                raise_to(level2, 1, None, send2.at[s])
                send(("up2", s), send2.at[s], recv2.at[s], y3_id)
            else:
                raise_to(level2, 1, own2.at[s], None)

    lift[...] = mm(ainv[...], cpl[...], NN).astype(BF16)

    for s in range(STREAMS):
        sent["up2", s].wait_recv()
        operand = live(own2[s] + recv2[s].astype(F32), 2).astype(BF16)
        solve(operand, 2, solved3.at[s])
        raise_to(solved3[s], 2, own3.at[s], send3.at[s])
        send(("up3", s), send3.at[s], recv3.at[s], x1_id)

    for n in tiles:
        pick_op[:, n : n + 256] = mm(select_t[...], finv[0, :, n : n + 256], TN).astype(BF16)

    sent["solved1"].wait_recv()
    for s in range(STREAMS):
        for q in range(4):
            at = slice((s * 4 + q) * w, (s * 4 + q + 1) * w)
            mine = solved1[at, :]
            other = solved1_other[at, :]
            both = jnp.concatenate(
                [jnp.where(c == 0, mine, other), jnp.where(c == 0, other, mine)], axis=0
            )
            base[s * 4 + q] = mm(both, select_t[...], NN).astype(BF16)

    for s in range(STREAMS):
        sent["up3", s].wait_recv()
        operand = live(own3[s] + recv3[s].astype(F32), 3).astype(BF16)
        solve(operand, 3, solved4.at[s])
        raise_to(solved4[s], 3, own4.at[s], send4.at[s])
        send(("up4", s), send4.at[s], recv4.at[s], x3_id)

    for s in range(STREAMS):
        sent["up4", s].wait_recv()
        operand = live(own4[s] + recv4[s].astype(F32), 4).astype(BF16)
        back5 = jnp.concatenate(
            [mm(operand, finv[4, n : n + 256, :], NT) for n in tiles], axis=1
        )
        back5 = live(back5, 4).astype(BF16)
        back4 = own4.at[s]
        lifted = jnp.concatenate(
            [mm(back5, fcpl[3, n : n + 256, :], NT).astype(BF16) for n in tiles], axis=1
        )
        back4 = jnp.concatenate(
            [
                solved4[s, :, n : n + 256].astype(F32) - mm(lifted, finv[3, n : n + 256, :], NT)
                for n in tiles
            ],
            axis=1,
        )
        back4 = live(back4, 3).astype(BF16)
        descend(back4, 2, solved3.at[s], back3.at[s])
        send(("down2", s), back3.at[s], back3_other.at[s], y3_id)
        descend(back3[s], 1, solved2.at[s, pl.ds(w, w)], back2.at[s, 3])
        send(("down1", s, 1), back2.at[s, 3], back2.at[s, 1], y1_id)
        send(("core", s, 3), back2.at[s, 3], back2_other.at[s, 3], core_id)

    def contribution(s, q):
        mine = back2[s, q]
        other = back2_other[s, q]
        both = jnp.concatenate(
            [jnp.where(c == 0, mine, other), jnp.where(c == 0, other, mine)], axis=0
        )
        lifted = jnp.concatenate(
            [mm(both, fcpl[0, n : n + 256, :], NT).astype(BF16) for n in tiles], axis=1
        )
        lane_live = lax.broadcasted_iota(jnp.int32, (1, bound), 1)
        picked = base[s * 4 + q].astype(F32) - mm(lifted, pick_op[...], NT) * alive[...]
        picked = picked.astype(BF16)

        def rows_of(shift):
            at = pl.multiple_of(lax.rem(z + shift, nz) * zrows, zrows)
            start = (s * 4 + q) * wide
            value = half[pl.ds(at, zrows), start : start + wide].astype(F32) - mm(
                lift[pl.ds(at, zrows), :], picked, NT
            )
            return weight_ref[0] * value

        return rows_of

    alive = jnp.where(rows_ref[...] < sizes_ref[0], 1.0, 0.0)
    hz = zrows // 2

    def scatter_first(k, s, q):
        rows_of = contribution(s, q)
        far = rows_of(2).astype(BF16)
        zsend1[k] = far
        send(("z1p", k), zsend1.at[k, pl.ds(0, hz)], zrecv1.at[k, pl.ds(0, hz)], zp_id)
        send(("z1m", k), zsend1.at[k, pl.ds(hz, hz)], zrecv1.at[k, pl.ds(hz, hz)], zm_id)
        zown[k, 1] = rows_of(1)
        zown[k, 2] = rows_of(3)
        zown[k, 0] = rows_of(0)

    def scatter_second(k):
        sent["z1p", k].wait_recv()
        zsend2[k, 0, :hz] = (zown[k, 1, :hz] + zrecv1[k, :hz].astype(F32)).astype(BF16)
        zsend2[k, 0, hz:] = zown[k, 1, hz:].astype(BF16)
        send(("z2p", k), zsend2.at[k, 0], zrecv2.at[k, 0], zp_id)
        sent["z1m", k].wait_recv()
        zsend2[k, 1, :hz] = zown[k, 2, :hz].astype(BF16)
        zsend2[k, 1, hz:] = (zown[k, 2, hz:] + zrecv1[k, hz:].astype(F32)).astype(BF16)
        send(("z2m", k), zsend2.at[k, 1], zrecv2.at[k, 1], zm_id)

    steps = []
    for q in (3, 2, 1, 0):
        for s in range(STREAMS):
            steps.append((s, q))
    for k, (s, q) in enumerate(steps):
        if q == 2:
            sent["down2", s].wait_recv()
            descend(back3_other[s], 1, solved2.at[s, pl.ds(0, w)], back2.at[s, 2])
            send(("down1", s, 0), back2.at[s, 2], back2.at[s, 0], y1_id)
            send(("core", s, 2), back2.at[s, 2], back2_other.at[s, 2], core_id)
        elif q < 2:
            sent["down1", s, q].wait_recv()
            send(("core", s, q), back2.at[s, q], back2_other.at[s, q], core_id)
        sent["core", s, q].wait_recv()
        scatter_first(k, s, q)
        if k:
            scatter_second(k - 1)
    scatter_second(len(steps) - 1)
    for k, (s, q) in enumerate(steps):
        sent["z2p", k].wait_recv()
        sent["z2m", k].wait_recv()
        out_ref[0, :, pl.ds(column(s, q), wide)] = (
            zown[k, 0] + zrecv2[k, 0].astype(F32) + zrecv2[k, 1].astype(F32)
        )
    for copy in sent.values():
        copy.wait_send()


def body(
    leaf_rhs,
    leaf_inverse,
    leaf_coupling,
    leaf_rows,
    front_sizes,
    front_inverse,
    front_coupling,
    shift_weight,
):
    order = leaf_inverse.shape[-1]
    columns = leaf_rhs.shape[-1]
    front = front_inverse.shape[-1]
    bound = leaf_coupling.shape[-1]
    wide = columns // (4 * STREAMS)
    w = wide // 2
    zrows = order // lax.axis_size("shift")
    pieces = 4 * STREAMS
    vmem = pltpu.VMEM
    hbm = pl.BlockSpec(memory_space=pl.ANY)
    local = pl.BlockSpec(memory_space=pltpu.VMEM)
    scalar = pl.BlockSpec(memory_space=pltpu.SMEM)
    level = lambda kind: vmem((STREAMS, w, front), kind)
    sends = 2 * STREAMS + 1 + 2 * STREAMS + 3 * STREAMS + STREAMS + 2 * STREAMS + 4 * STREAMS
    sends += 4 * pieces
    return pl.pallas_call(
        kernel,
        out_shape=jax.ShapeDtypeStruct((1, zrows, columns), F32),
        in_specs=[hbm, hbm, hbm, local, scalar, hbm, hbm, scalar],
        out_specs=local,
        scratch_shapes=[
            vmem((order, columns), BF16),
            vmem((order, order), BF16),
            vmem((order, bound), BF16),
            vmem((5, front, front), BF16),
            vmem((4, front, front), BF16),
            vmem((front, bound), BF16),
            vmem((bound, order), BF16),
            vmem((order, columns), BF16),
            vmem((order, bound), BF16),
            vmem((bound, front), BF16),
            vmem((STREAMS, 4 * w, front), F32),
            vmem((STREAMS, 4 * w, front), BF16),
            vmem((STREAMS, 4 * w, front), BF16),
            vmem((STREAMS * 4 * w, front), BF16),
            vmem((STREAMS * 4 * w, front), BF16),
            vmem((pieces, wide, bound), BF16),
            vmem((STREAMS, 2 * w, front), F32),
            vmem((STREAMS, 2 * w, front), BF16),
            vmem((STREAMS, 2 * w, front), BF16),
            vmem((STREAMS, 2 * w, front), BF16),
            level(F32),
            level(BF16),
            level(BF16),
            level(BF16),
            level(F32),
            level(BF16),
            level(BF16),
            level(BF16),
            level(F32),
            level(BF16),
            level(BF16),
            level(BF16),
            level(BF16),
            vmem((STREAMS, 4, w, front), BF16),
            vmem((STREAMS, 4, w, front), BF16),
            vmem((pieces, 3, zrows, wide), F32),
            vmem((pieces, zrows, wide), BF16),
            vmem((pieces, zrows, wide), BF16),
            vmem((pieces, 2, zrows, wide), BF16),
            vmem((pieces, 2, zrows, wide), BF16),
            pltpu.SemaphoreType.DMA((2 + pieces + 9,)),
            pltpu.SemaphoreType.DMA((sends,)),
            pltpu.SemaphoreType.DMA((sends,)),
        ],
        compiler_params=pltpu.CompilerParams(
            collective_id=0, has_side_effects=True, vmem_limit_bytes=60 * 2**20
        ),
    )(
        leaf_rhs,
        leaf_inverse,
        leaf_coupling,
        leaf_rows,
        front_sizes,
        front_inverse,
        front_coupling,
        shift_weight,
    )


def solution(mesh):
    in_specs = (
        P("leaf", None, None),
        P("shift", "leaf", None, None),
        P("shift", "leaf", None, None),
        P("leaf", None),
        P(),
        P("shift", None, "leaf", None, None),
        P("shift", None, "leaf", None, None),
        P("shift"),
    )
    out_specs = P("leaf", "shift", None)
    return jax.shard_map(body, mesh=mesh, in_specs=in_specs, out_specs=out_specs, check_vma=False)
```

```python
import jax
import jax.numpy as jnp
from jax import lax
from jax.experimental import pallas as pl
from jax.experimental.pallas import tpu as pltpu
from jax.sharding import PartitionSpec as P

F32 = jnp.float32
BF16 = jnp.bfloat16
NN = (((1,), (0,)), ((), ()))
NT = (((1,), (1,)), ((), ()))
TN = (((0,), (0,)), ((), ()))
STREAMS = 2


def mm(left, right, dims):
    return lax.dot_general(left, right, dims, preferred_element_type=F32)


def kernel(
    rhs_hbm,
    ainv_hbm,
    cpl_hbm,
    rows_ref,
    sizes_ref,
    finv_hbm,
    fcpl_hbm,
    weight_ref,
    out_ref,
    rhs,
    ainv,
    cpl,
    cpl_t,
    finv,
    fcpl,
    select,
    select_t,
    half,
    lift,
    pick_op,
    placed,
    recv0,
    solved1,
    base,
    own1,
    send1,
    recv1,
    solved2,
    own2,
    send2,
    recv2,
    solved3,
    own3,
    send3,
    recv3,
    solved4,
    own4,
    send4,
    recv4,
    back3,
    back3_other,
    back2,
    zown,
    zsend1,
    zrecv1,
    zsend2,
    zrecv2,
    load_sem,
    send_sem,
    recv_sem,
):
    leaf_order, _ = ainv.shape
    front = finv.shape[-1]
    bound = cpl.shape[-1]
    wide = rhs.shape[-1] // (4 * STREAMS)
    w = wide // 2
    zrows = out_ref.shape[1]
    nz = leaf_order // zrows

    p = lax.axis_index("leaf")
    z = lax.axis_index("shift")
    c = lax.rem(p, 2)
    y = lax.rem(p // 2, 4)
    x = p // 8
    h2 = y // 2
    h1 = lax.rem(lax.rem(y, 2) + h2, 2)

    def leaf_of(xx, yy, cc):
        return {"leaf": (xx * 4 + yy) * 2 + cc}

    core_id = leaf_of(x, y, 1 - c)
    y1_id = leaf_of(x, y + 1 - 2 * lax.rem(y, 2), c)
    y3_id = leaf_of(x, 3 - y, c)
    x1_id = leaf_of(x + 1 - 2 * lax.rem(x, 2), y, c)
    x3_id = leaf_of(3 - x, y, c)
    zp_id = {"shift": lax.rem(z + 1, nz)}
    zm_id = {"shift": lax.rem(z + nz - 1, nz)}
    halves = ((1 - h1, 1 - h2), (1 - h1, h2), (h1, 1 - h2), (h1, h2))

    barrier = pltpu.get_barrier_semaphore()
    partners = (core_id, y1_id, y3_id, x1_id, x3_id, zp_id, zm_id)
    for partner in partners:
        pl.semaphore_signal(
            barrier, inc=1, device_id=partner, device_id_type=pl.DeviceIdType.MESH
        )

    def column(s, q):
        a, b = halves[q]
        return pl.multiple_of(((a * 2 + b) * STREAMS + s) * wide, wide)

    loads = {}

    def load(name, src, dst):
        copy = pltpu.make_async_copy(src, dst, load_sem.at[len(loads)])
        loads[name] = copy
        copy.start()

    def load_rhs(s, pair):
        for q in (2 * pair, 2 * pair + 1):
            load(
                ("rhs", s, q),
                rhs_hbm.at[0, :, pl.ds(column(s, q), wide)],
                rhs.at[:, pl.ds((s * 4 + q) * wide, wide)],
            )

    def load_level(level):
        load(("finv", level), finv_hbm.at[0, level, 0], finv.at[level])
        if level < 4:
            load(("fcpl", level), fcpl_hbm.at[0, level, 0], fcpl.at[level])

    load("cpl", cpl_hbm.at[0, 0], cpl)
    load_rhs(0, 0)
    load("ainv", ainv_hbm.at[0, 0], ainv)
    load_rhs(1, 0)
    load_level(0)

    sent = {}

    def send(name, src, dst, device):
        copy = pltpu.make_async_remote_copy(
            src_ref=src,
            dst_ref=dst,
            send_sem=send_sem.at[len(sent)],
            recv_sem=recv_sem.at[len(sent)],
            device_id=device,
            device_id_type=pl.DeviceIdType.MESH,
        )
        sent[name] = copy
        copy.start()

    def live(value, level):
        lane = lax.broadcasted_iota(jnp.int32, value.shape, len(value.shape) - 1)
        return jnp.where(lane < sizes_ref[level], value, 0.0)

    tiles = range(0, front, 256)

    def solve(operand, level, dst):
        for n in tiles:
            got = mm(operand, finv[level, n : n + 256, :], NT)
            lane = n + lax.broadcasted_iota(jnp.int32, got.shape, 1)
            got = jnp.where(lane < sizes_ref[level], got, 0.0).astype(BF16)
            dst(n, got)

    def into(ref):
        def put(n, got):
            ref[:, n : n + 256] = got

        return put

    def raise_to(solved, level, keep, out):
        for n in tiles:
            got = mm(solved, fcpl[level, :, n : n + 256], NN)
            if keep is not None:
                keep[:, n : n + 256] = got
            if out is not None:
                out[:, n : n + 256] = got.astype(BF16)

    def descend(parent, level, solved, dst):
        lifted = jnp.concatenate(
            [mm(parent, fcpl[level, n : n + 256, :], NT).astype(BF16) for n in tiles], axis=1
        )
        for n in tiles:
            got = solved[:, n : n + 256].astype(F32) - mm(
                lifted, finv[level, n : n + 256, :], NT
            )
            lane = n + lax.broadcasted_iota(jnp.int32, got.shape, 1)
            dst[:, n : n + 256] = jnp.where(lane < sizes_ref[level], got, 0.0).astype(BF16)

    for n in tiles:
        row = n + lax.broadcasted_iota(jnp.int32, (256, bound), 0)
        chosen = jnp.where(row == rows_ref[...], 1.0, 0.0)
        select_t[n : n + 256, :] = chosen.astype(BF16)
        select[:, n : n + 256] = jnp.transpose(chosen).astype(BF16)

    loads["cpl"].wait()
    cpl_t[...] = jnp.transpose(cpl[...])

    def halve(s, pair):
        loads["rhs", s, 2 * pair].wait()
        loads["rhs", s, 2 * pair + 1].wait()
        start = (s * 4 + 2 * pair) * wide
        half[:, start : start + 2 * wide] = mm(
            ainv[...], rhs[:, start : start + 2 * wide], NN
        ).astype(BF16)

    def place(s, pair):
        start = (s * 4 + 2 * pair) * wide
        boundary = mm(cpl_t[...], half[:, start : start + 2 * wide], NN)
        boundary_t = jnp.transpose(boundary).astype(BF16)
        for n in tiles:
            got = mm(boundary_t, select_t[n : n + 256, :], NT).astype(BF16)
            for q in range(2):
                for core in range(2):
                    at = (2 * q + core) * w
                    placed[s, pair, core, q * w : q * w + w, n : n + 256] = got[at : at + w]
        send(("place", s, pair), placed.at[s, pair, 1 - c], recv0.at[s, pair], core_id)

    def first(s, pair):
        sent["place", s, pair].wait_recv()
        gathered = placed[s, pair, c].astype(F32) + recv0[s, pair].astype(F32)
        operand = live(gathered, 0).astype(BF16)
        got = []

        def put(n, value):
            got.append(value)
            for q in range(2):
                solved1[s * 4 + 2 * pair + q, c, :, n : n + 256] = value[q * w : q * w + w]

        solve(operand, 0, put)
        level1 = jnp.concatenate(got, axis=1)
        if pair == 0:
            raise_to(level1, 0, None, send1.at[s])
            for q in range(2):
                at = pl.ds(q * w, w)
                send(("up1", s, q), send1.at[s, at], recv1.at[s, at], y1_id)
        else:
            raise_to(level1, 0, own1.at[s], None)
        for q in range(2):
            piece = solved1.at[s * 4 + 2 * pair + q, c]
            send(("solved1", s, 2 * pair + q), piece, piece, core_id)

    def second(s, q):
        sent["up1", s, q].wait_recv()
        at = slice(q * w, q * w + w)
        operand = live(own1[s, at, :] + recv1[s, at, :].astype(F32), 1).astype(BF16)
        solve(operand, 1, into(solved2.at[s, pl.ds(q * w, w)]))
        level2 = solved2[s, at, :]
        if q == 0:
            raise_to(level2, 1, None, send2.at[s])
            send(("up2", s), send2.at[s], recv2.at[s], y3_id)
        else:
            raise_to(level2, 1, own2.at[s], None)

    def third(s):
        sent["up2", s].wait_recv()
        operand = live(own2[s] + recv2[s].astype(F32), 2).astype(BF16)
        solve(operand, 2, into(solved3.at[s]))
        raise_to(solved3[s], 2, own3.at[s], send3.at[s])
        send(("up3", s), send3.at[s], recv3.at[s], x1_id)

    def fourth(s):
        sent["up3", s].wait_recv()
        operand = live(own3[s] + recv3[s].astype(F32), 3).astype(BF16)
        solve(operand, 3, into(solved4.at[s]))
        raise_to(solved4[s], 3, own4.at[s], send4.at[s])
        send(("up4", s), send4.at[s], recv4.at[s], x3_id)

    def turn(s):
        sent["up4", s].wait_recv()
        operand = live(own4[s] + recv4[s].astype(F32), 4).astype(BF16)
        got = []
        solve(operand, 4, lambda n, value: got.append(value))
        back5 = jnp.concatenate(got, axis=1)
        lifted = jnp.concatenate(
            [mm(back5, fcpl[3, n : n + 256, :], NT).astype(BF16) for n in tiles], axis=1
        )
        back4 = jnp.concatenate(
            [
                solved4[s, :, n : n + 256].astype(F32) - mm(lifted, finv[3, n : n + 256, :], NT)
                for n in tiles
            ],
            axis=1,
        )
        back4 = live(back4, 3).astype(BF16)
        descend(back4, 2, solved3.at[s], back3.at[s])
        send(("down2", s), back3.at[s], back3_other.at[s], y3_id)
        descend(back3[s], 1, solved2.at[s, pl.ds(w, w)], back2.at[s, 3, c])
        spread(s, 3)

    def spread(s, q):
        piece = back2.at[s, q, c]
        if q >= 2:
            send(("down1", s, q - 2), piece, back2.at[s, q - 2, c], y1_id)
        send(("core", s, q), piece, piece, core_id)

    def lower(s):
        sent["down2", s].wait_recv()
        descend(back3_other[s], 1, solved2.at[s, pl.ds(0, w)], back2.at[s, 2, c])
        spread(s, 2)

    hz = zrows // 2

    def scatter_first(k, s, q):
        both = back2[s, q].reshape(wide, front)
        picked = base[s * 4 + q].astype(F32) - mm(both, pick_op[...], NT)
        picked = picked.astype(BF16)
        start = (s * 4 + q) * wide

        def rows_of(shift):
            at = pl.multiple_of(lax.rem(z + shift, nz) * zrows, zrows)
            value = half[pl.ds(at, zrows), start : start + wide].astype(F32) - mm(
                lift[pl.ds(at, zrows), :], picked, NT
            )
            return weight_ref[0] * value

        zsend1[k] = rows_of(2).astype(BF16)
        send(("z1p", k), zsend1.at[k, pl.ds(0, hz)], zrecv1.at[k, pl.ds(0, hz)], zp_id)
        send(("z1m", k), zsend1.at[k, pl.ds(hz, hz)], zrecv1.at[k, pl.ds(hz, hz)], zm_id)
        zown[k, 1] = rows_of(1)
        zown[k, 2] = rows_of(3)
        zown[k, 0] = rows_of(0)

    def scatter_second(k):
        sent["z1p", k].wait_recv()
        zsend2[k, 0, :hz] = (zown[k, 1, :hz] + zrecv1[k, :hz].astype(F32)).astype(BF16)
        zsend2[k, 0, hz:] = zown[k, 1, hz:].astype(BF16)
        send(("z2p", k), zsend2.at[k, 0], zrecv2.at[k, 0], zp_id)
        sent["z1m", k].wait_recv()
        zsend2[k, 1, :hz] = zown[k, 2, :hz].astype(BF16)
        zsend2[k, 1, hz:] = (zown[k, 2, hz:] + zrecv1[k, hz:].astype(F32)).astype(BF16)
        send(("z2m", k), zsend2.at[k, 1], zrecv2.at[k, 1], zm_id)

    steps = []

    def step(s, q):
        if q < 2:
            sent["down1", s, q].wait_recv()
            send(("core", s, q), back2.at[s, q, c], back2.at[s, q, c], core_id)
        sent["core", s, q].wait_recv()
        k = len(steps)
        steps.append((s, q))
        scatter_first(k, s, q)
        if k:
            scatter_second(k - 1)

    def make_lift():
        lift[...] = mm(ainv[...], cpl[...], NN).astype(BF16)

    def make_pick():
        row = [mm(live(select[...], 0), finv[0, :, n : n + 256], NN).astype(BF16) for n in tiles]
        row = jnp.concatenate(row, axis=1)
        for n in tiles:
            pick_op[:, n : n + 256] = mm(row, fcpl[0, :, n : n + 256], NN).astype(BF16)

    def make_base(s):
        for q in range(4):
            sent["solved1", s, q].wait_recv()
        at = slice(s * 4, s * 4 + 4)
        got = mm(solved1[at].reshape(4 * wide, front), select_t[...], NN).astype(BF16)
        base[at] = got.reshape(4, wide, bound)

    loads["ainv"].wait()
    halve(0, 0)
    load_rhs(0, 1)
    load_rhs(1, 1)
    pl.semaphore_wait(barrier, len(partners))
    place(0, 0)
    for level in range(1, 5):
        load_level(level)
    halve(1, 0)
    loads["finv", 0].wait()
    loads["fcpl", 0].wait()
    first(0, 0)
    place(1, 0)
    halve(0, 1)
    first(1, 0)
    place(0, 1)
    halve(1, 1)
    first(0, 1)
    loads["finv", 1].wait()
    loads["fcpl", 1].wait()
    second(0, 0)
    place(1, 1)
    second(0, 1)
    first(1, 1)
    for level in range(2, 5):
        loads["finv", level].wait()
        if level < 4:
            loads["fcpl", level].wait()
    second(1, 0)
    third(0)
    second(1, 1)
    make_lift()
    third(1)
    make_pick()
    fourth(0)
    make_base(0)
    make_base(1)
    fourth(1)
    turn(0)
    step(0, 3)
    turn(1)
    lower(0)
    step(0, 2)
    step(0, 1)
    step(1, 3)
    lower(1)
    step(0, 0)
    step(1, 2)
    step(1, 1)
    step(1, 0)
    scatter_second(len(steps) - 1)
    for k, (s, q) in enumerate(steps):
        sent["z2p", k].wait_recv()
        sent["z2m", k].wait_recv()
        out_ref[0, :, pl.ds(column(s, q), wide)] = (
            zown[k, 0] + zrecv2[k, 0].astype(F32) + zrecv2[k, 1].astype(F32)
        )
    for copy in sent.values():
        copy.wait_send()


def body(
    leaf_rhs,
    leaf_inverse,
    leaf_coupling,
    leaf_rows,
    front_sizes,
    front_inverse,
    front_coupling,
    shift_weight,
):
    order = leaf_inverse.shape[-1]
    columns = leaf_rhs.shape[-1]
    front = front_inverse.shape[-1]
    bound = leaf_coupling.shape[-1]
    wide = columns // (4 * STREAMS)
    w = wide // 2
    zrows = order // lax.axis_size("shift")
    pieces = 4 * STREAMS
    vmem = pltpu.VMEM
    hbm = pl.BlockSpec(memory_space=pl.ANY)
    local = pl.BlockSpec(memory_space=pltpu.VMEM)
    scalar = pl.BlockSpec(memory_space=pltpu.SMEM)
    level = lambda kind: vmem((STREAMS, w, front), kind)
    sends = 18 * STREAMS + 4 * pieces
    return pl.pallas_call(
        kernel,
        out_shape=jax.ShapeDtypeStruct((1, zrows, columns), F32),
        in_specs=[hbm, hbm, hbm, local, scalar, hbm, hbm, scalar],
        out_specs=local,
        scratch_shapes=[
            vmem((order, columns), BF16),
            vmem((order, order), BF16),
            vmem((order, bound), BF16),
            vmem((bound, order), BF16),
            vmem((5, front, front), BF16),
            vmem((4, front, front), BF16),
            vmem((bound, front), BF16),
            vmem((front, bound), BF16),
            vmem((order, columns), BF16),
            vmem((order, bound), BF16),
            vmem((bound, front), BF16),
            vmem((STREAMS, 2, 2, 2 * w, front), BF16),
            vmem((STREAMS, 2, 2 * w, front), BF16),
            vmem((pieces, 2, w, front), BF16),
            vmem((pieces, wide, bound), BF16),
            vmem((STREAMS, 2 * w, front), F32),
            vmem((STREAMS, 2 * w, front), BF16),
            vmem((STREAMS, 2 * w, front), BF16),
            vmem((STREAMS, 2 * w, front), BF16),
            level(F32),
            level(BF16),
            level(BF16),
            level(BF16),
            level(F32),
            level(BF16),
            level(BF16),
            level(BF16),
            level(F32),
            level(BF16),
            level(BF16),
            level(BF16),
            level(BF16),
            vmem((STREAMS, 4, 2, w, front), BF16),
            vmem((pieces, 3, zrows, wide), F32),
            vmem((pieces, zrows, wide), BF16),
            vmem((pieces, zrows, wide), BF16),
            vmem((pieces, 2, zrows, wide), BF16),
            vmem((pieces, 2, zrows, wide), BF16),
            pltpu.SemaphoreType.DMA((2 + pieces + 9,)),
            pltpu.SemaphoreType.DMA((sends,)),
            pltpu.SemaphoreType.DMA((sends,)),
        ],
        compiler_params=pltpu.CompilerParams(
            collective_id=0, has_side_effects=True, vmem_limit_bytes=60 * 2**20
        ),
    )(
        leaf_rhs,
        leaf_inverse,
        leaf_coupling,
        leaf_rows,
        front_sizes,
        front_inverse,
        front_coupling,
        shift_weight,
    )


def solution(mesh):
    in_specs = (
        P("leaf", None, None),
        P("shift", "leaf", None, None),
        P("shift", "leaf", None, None),
        P("leaf", None),
        P(),
        P("shift", None, "leaf", None, None),
        P("shift", None, "leaf", None, None),
        P("shift"),
    )
    out_specs = P("leaf", "shift", None)
    return jax.shard_map(body, mesh=mesh, in_specs=in_specs, out_specs=out_specs, check_vma=False)
```

```python
import jax
import jax.numpy as jnp
from jax import lax
from jax.experimental import pallas as pl
from jax.experimental.pallas import tpu as pltpu
from jax.sharding import PartitionSpec as P

F32 = jnp.float32
BF16 = jnp.bfloat16
NN = (((1,), (0,)), ((), ()))
NT = (((1,), (1,)), ((), ()))
TN = (((0,), (0,)), ((), ()))
STREAMS = 2


def mm(left, right, dims):
    return lax.dot_general(left, right, dims, preferred_element_type=F32)


def kernel(
    rhs_hbm,
    ainv_hbm,
    cpl_hbm,
    rows_hbm,
    sizes_hbm,
    finv_hbm,
    fcpl_hbm,
    weight_ref,
    out_ref,
    rows_ref,
    sizes_ref,
    rhs,
    ainv,
    cpl,
    cpl_t,
    finv,
    fcpl,
    select,
    select_t,
    half,
    lift,
    pick_op,
    placed,
    recv0,
    solved1,
    base,
    own1,
    send1,
    recv1,
    solved2,
    own2,
    send2,
    recv2,
    solved3,
    own3,
    send3,
    recv3,
    solved4,
    own4,
    send4,
    recv4,
    back3,
    back3_other,
    back2,
    zown,
    zsend1,
    zrecv1,
    zsend2,
    zrecv2,
    load_sem,
    send_sem,
    recv_sem,
):
    leaf_order, _ = ainv.shape
    front = finv.shape[-1]
    bound = cpl.shape[-1]
    wide = rhs.shape[-1] // (4 * STREAMS)
    w = wide // 2
    zrows = out_ref.shape[1]
    nz = leaf_order // zrows

    p = lax.axis_index("leaf")
    z = lax.axis_index("shift")
    c = lax.rem(p, 2)
    y = lax.rem(p // 2, 4)
    x = p // 8
    h2 = y // 2
    h1 = lax.rem(lax.rem(y, 2) + h2, 2)

    def leaf_of(xx, yy, cc):
        return {"leaf": (xx * 4 + yy) * 2 + cc}

    core_id = leaf_of(x, y, 1 - c)
    y1_id = leaf_of(x, y + 1 - 2 * lax.rem(y, 2), c)
    y3_id = leaf_of(x, 3 - y, c)
    x1_id = leaf_of(x + 1 - 2 * lax.rem(x, 2), y, c)
    x3_id = leaf_of(3 - x, y, c)
    zp_id = {"shift": lax.rem(z + 1, nz)}
    zm_id = {"shift": lax.rem(z + nz - 1, nz)}
    halves = ((1 - h1, 1 - h2), (1 - h1, h2), (h1, 1 - h2), (h1, h2))

    barrier = pltpu.get_barrier_semaphore()
    partners = (core_id, y1_id, y3_id, x1_id, x3_id, zp_id, zm_id)
    for partner in partners:
        pl.semaphore_signal(
            barrier, inc=1, device_id=partner, device_id_type=pl.DeviceIdType.MESH
        )

    def column(s, q):
        a, b = halves[q]
        return pl.multiple_of(((a * 2 + b) * STREAMS + s) * wide, wide)

    loads = {}

    def load(name, src, dst):
        copy = pltpu.make_async_copy(src, dst, load_sem.at[len(loads)])
        loads[name] = copy
        copy.start()

    def load_rhs(s, pair):
        for q in (2 * pair, 2 * pair + 1):
            load(
                ("rhs", s, q),
                rhs_hbm.at[0, :, pl.ds(column(s, q), wide)],
                rhs.at[:, pl.ds((s * 4 + q) * wide, wide)],
            )

    def load_level(level):
        load(("finv", level), finv_hbm.at[0, level, 0], finv.at[level])
        if level < 4:
            load(("fcpl", level), fcpl_hbm.at[0, level, 0], fcpl.at[level])

    load("rows", rows_hbm, rows_ref)
    load("cpl", cpl_hbm.at[0, 0], cpl)
    load("sizes", sizes_hbm, sizes_ref)
    load_rhs(0, 0)
    load("ainv", ainv_hbm.at[0, 0], ainv)
    load_rhs(1, 0)
    load_level(0)

    sent = {}

    def send(name, src, dst, device):
        copy = pltpu.make_async_remote_copy(
            src_ref=src,
            dst_ref=dst,
            send_sem=send_sem.at[len(sent)],
            recv_sem=recv_sem.at[len(sent)],
            device_id=device,
            device_id_type=pl.DeviceIdType.MESH,
        )
        sent[name] = copy
        copy.start()

    def live(value, level):
        lane = lax.broadcasted_iota(jnp.int32, value.shape, len(value.shape) - 1)
        return jnp.where(lane < sizes_ref[level], value, 0.0)

    tiles = range(0, front, 256)

    def solve(operand, level, dst):
        for n in tiles:
            got = mm(operand, finv[level, n : n + 256, :], NT)
            lane = n + lax.broadcasted_iota(jnp.int32, got.shape, 1)
            got = jnp.where(lane < sizes_ref[level], got, 0.0).astype(BF16)
            dst(n, got)

    def into(ref):
        def put(n, got):
            ref[:, n : n + 256] = got

        return put

    def raise_to(solved, level, keep, out):
        for n in tiles:
            got = mm(solved, fcpl[level, :, n : n + 256], NN)
            if keep is not None:
                keep[:, n : n + 256] = got
            if out is not None:
                out[:, n : n + 256] = got.astype(BF16)

    def descend(parent, level, solved, dst):
        lifted = jnp.concatenate(
            [mm(parent, fcpl[level, n : n + 256, :], NT).astype(BF16) for n in tiles], axis=1
        )
        for n in tiles:
            got = solved[:, n : n + 256].astype(F32) - mm(
                lifted, finv[level, n : n + 256, :], NT
            )
            lane = n + lax.broadcasted_iota(jnp.int32, got.shape, 1)
            dst[:, n : n + 256] = jnp.where(lane < sizes_ref[level], got, 0.0).astype(BF16)

    loads["rows"].wait()
    for n in tiles:
        row = n + lax.broadcasted_iota(jnp.int32, (256, bound), 0)
        chosen = jnp.where(row == rows_ref[...], 1.0, 0.0)
        select_t[n : n + 256, :] = chosen.astype(BF16)
        select[:, n : n + 256] = jnp.transpose(chosen).astype(BF16)

    loads["cpl"].wait()
    cpl_t[...] = jnp.transpose(cpl[...])

    def halve(s, pair):
        loads["rhs", s, 2 * pair].wait()
        loads["rhs", s, 2 * pair + 1].wait()
        start = (s * 4 + 2 * pair) * wide
        half[:, start : start + 2 * wide] = mm(
            ainv[...], rhs[:, start : start + 2 * wide], NN
        ).astype(BF16)

    def place(s, pair):
        start = (s * 4 + 2 * pair) * wide
        boundary = mm(cpl_t[...], half[:, start : start + 2 * wide], NN)
        boundary_t = jnp.transpose(boundary).astype(BF16)
        for n in tiles:
            got = mm(boundary_t, select_t[n : n + 256, :], NT).astype(BF16)
            for q in range(2):
                for core in range(2):
                    at = (2 * q + core) * w
                    placed[s, pair, core, q * w : q * w + w, n : n + 256] = got[at : at + w]

    def send_place(s, pair):
        send(("place", s, pair), placed.at[s, pair, 1 - c], recv0.at[s, pair], core_id)

    def first(s, pair):
        sent["place", s, pair].wait_recv()
        gathered = placed[s, pair, c].astype(F32) + recv0[s, pair].astype(F32)
        operand = live(gathered, 0).astype(BF16)
        got = []

        def put(n, value):
            got.append(value)
            for q in range(2):
                solved1[s * 4 + 2 * pair + q, c, :, n : n + 256] = value[q * w : q * w + w]

        solve(operand, 0, put)
        level1 = jnp.concatenate(got, axis=1)
        if pair == 0:
            raise_to(level1, 0, None, send1.at[s])
            send_up1(s, 0)
        else:
            raise_to(level1, 0, own1.at[s], None)
        for q in range(2):
            piece = solved1.at[s * 4 + 2 * pair + q, c]
            send(("solved1", s, 2 * pair + q), piece, piece, core_id)

    def send_up1(s, q):
        at = pl.ds(q * w, w)
        send(("up1", s, q), send1.at[s, at], recv1.at[s, at], y1_id)

    def second(s, q):
        sent["up1", s, q].wait_recv()
        at = slice(q * w, q * w + w)
        operand = live(own1[s, at, :] + recv1[s, at, :].astype(F32), 1).astype(BF16)
        solve(operand, 1, into(solved2.at[s, pl.ds(q * w, w)]))
        level2 = solved2[s, at, :]
        if q == 0:
            raise_to(level2, 1, None, send2.at[s])
            send(("up2", s), send2.at[s], recv2.at[s], y3_id)
        else:
            raise_to(level2, 1, own2.at[s], None)

    def third(s):
        sent["up2", s].wait_recv()
        operand = live(own2[s] + recv2[s].astype(F32), 2).astype(BF16)
        solve(operand, 2, into(solved3.at[s]))
        raise_to(solved3[s], 2, own3.at[s], send3.at[s])
        send(("up3", s), send3.at[s], recv3.at[s], x1_id)

    def fourth(s):
        sent["up3", s].wait_recv()
        operand = live(own3[s] + recv3[s].astype(F32), 3).astype(BF16)
        solve(operand, 3, into(solved4.at[s]))
        raise_to(solved4[s], 3, own4.at[s], send4.at[s])
        send(("up4", s), send4.at[s], recv4.at[s], x3_id)

    def turn(s):
        sent["up4", s].wait_recv()
        operand = live(own4[s] + recv4[s].astype(F32), 4).astype(BF16)
        got = []
        solve(operand, 4, lambda n, value: got.append(value))
        back5 = jnp.concatenate(got, axis=1)
        lifted = jnp.concatenate(
            [mm(back5, fcpl[3, n : n + 256, :], NT).astype(BF16) for n in tiles], axis=1
        )
        back4 = jnp.concatenate(
            [
                solved4[s, :, n : n + 256].astype(F32) - mm(lifted, finv[3, n : n + 256, :], NT)
                for n in tiles
            ],
            axis=1,
        )
        back4 = live(back4, 3).astype(BF16)
        descend(back4, 2, solved3.at[s], back3.at[s])
        send(("down2", s), back3.at[s], back3_other.at[s], y3_id)
        descend(back3[s], 1, solved2.at[s, pl.ds(w, w)], back2.at[s, 3, c])
        spread(s, 3)

    def spread(s, q):
        piece = back2.at[s, q, c]
        if q >= 2:
            send(("down1", s, q - 2), piece, back2.at[s, q - 2, c], y1_id)
        send(("core", s, q), piece, piece, core_id)

    def lower(s):
        sent["down2", s].wait_recv()
        descend(back3_other[s], 1, solved2.at[s, pl.ds(0, w)], back2.at[s, 2, c])
        spread(s, 2)

    hz = zrows // 2

    def scatter_first(k, s, q):
        both = back2[s, q].reshape(wide, front)
        picked = base[s * 4 + q].astype(F32) - mm(both, pick_op[...], NT)
        picked = picked.astype(BF16)
        start = (s * 4 + q) * wide

        def rows_of(shift):
            at = pl.multiple_of(lax.rem(z + shift, nz) * zrows, zrows)
            value = half[pl.ds(at, zrows), start : start + wide].astype(F32) - mm(
                lift[pl.ds(at, zrows), :], picked, NT
            )
            return weight_ref[0] * value

        zsend1[k] = rows_of(2).astype(BF16)
        send(("z1p", k), zsend1.at[k, pl.ds(0, hz)], zrecv1.at[k, pl.ds(0, hz)], zp_id)
        send(("z1m", k), zsend1.at[k, pl.ds(hz, hz)], zrecv1.at[k, pl.ds(hz, hz)], zm_id)
        zown[k, 1] = rows_of(1)
        zown[k, 2] = rows_of(3)
        zown[k, 0] = rows_of(0)

    def scatter_second(k):
        sent["z1p", k].wait_recv()
        zsend2[k, 0, :hz] = (zown[k, 1, :hz] + zrecv1[k, :hz].astype(F32)).astype(BF16)
        zsend2[k, 0, hz:] = zown[k, 1, hz:].astype(BF16)
        send(("z2p", k), zsend2.at[k, 0], zrecv2.at[k, 0], zp_id)
        sent["z1m", k].wait_recv()
        zsend2[k, 1, :hz] = zown[k, 2, :hz].astype(BF16)
        zsend2[k, 1, hz:] = (zown[k, 2, hz:] + zrecv1[k, hz:].astype(F32)).astype(BF16)
        send(("z2m", k), zsend2.at[k, 1], zrecv2.at[k, 1], zm_id)

    steps = []

    def step(s, q):
        if q < 2:
            sent["down1", s, q].wait_recv()
            send(("core", s, q), back2.at[s, q, c], back2.at[s, q, c], core_id)
        sent["core", s, q].wait_recv()
        k = len(steps)
        steps.append((s, q))
        scatter_first(k, s, q)
        if k > 1:
            scatter_second(k - 2)

    def make_lift():
        lift[...] = mm(ainv[...], cpl[...], NN).astype(BF16)

    def make_pick():
        row = [mm(live(select[...], 0), finv[0, :, n : n + 256], NN).astype(BF16) for n in tiles]
        row = jnp.concatenate(row, axis=1)
        for n in tiles:
            pick_op[:, n : n + 256] = mm(row, fcpl[0, :, n : n + 256], NN).astype(BF16)

    def make_base(s):
        for q in range(4):
            sent["solved1", s, q].wait_recv()
        at = slice(s * 4, s * 4 + 4)
        got = mm(solved1[at].reshape(4 * wide, front), select_t[...], NN).astype(BF16)
        base[at] = got.reshape(4, wide, bound)

    loads["sizes"].wait()
    loads["ainv"].wait()
    halve(0, 0)
    load_rhs(0, 1)
    load_rhs(1, 1)
    place(0, 0)
    for level in range(1, 5):
        load_level(level)
    halve(1, 0)
    place(1, 0)
    halve(0, 1)
    pl.semaphore_wait(barrier, len(partners))
    send_place(0, 0)
    send_place(1, 0)
    loads["finv", 0].wait()
    loads["fcpl", 0].wait()
    place(0, 1)
    send_place(0, 1)
    first(0, 0)
    first(1, 0)
    send_up1(0, 1)
    send_up1(1, 1)
    halve(1, 1)
    first(0, 1)
    place(1, 1)
    send_place(1, 1)
    loads["finv", 1].wait()
    loads["fcpl", 1].wait()
    second(0, 0)
    first(1, 1)
    second(1, 0)
    second(0, 1)
    for level in range(2, 5):
        loads["finv", level].wait()
        if level < 4:
            loads["fcpl", level].wait()
    third(0)
    second(1, 1)
    make_lift()
    third(1)
    make_pick()
    fourth(0)
    fourth(1)
    turn(0)
    make_base(0)
    make_base(1)
    turn(1)
    step(0, 3)
    lower(0)
    step(1, 3)
    lower(1)
    step(0, 2)
    step(0, 1)
    step(1, 2)
    step(1, 1)
    step(0, 0)
    step(1, 0)
    scatter_second(len(steps) - 2)
    scatter_second(len(steps) - 1)
    for k, (s, q) in enumerate(steps):
        sent["z2p", k].wait_recv()
        sent["z2m", k].wait_recv()
        out_ref[0, :, pl.ds(column(s, q), wide)] = (
            zown[k, 0] + zrecv2[k, 0].astype(F32) + zrecv2[k, 1].astype(F32)
        )
    for copy in sent.values():
        copy.wait_send()


def body(
    leaf_rhs,
    leaf_inverse,
    leaf_coupling,
    leaf_rows,
    front_sizes,
    front_inverse,
    front_coupling,
    shift_weight,
):
    order = leaf_inverse.shape[-1]
    columns = leaf_rhs.shape[-1]
    front = front_inverse.shape[-1]
    bound = leaf_coupling.shape[-1]
    wide = columns // (4 * STREAMS)
    w = wide // 2
    zrows = order // lax.axis_size("shift")
    pieces = 4 * STREAMS
    vmem = pltpu.VMEM
    hbm = pl.BlockSpec(memory_space=pltpu.HBM)
    local = pl.BlockSpec(memory_space=pltpu.VMEM)
    level = lambda kind: vmem((STREAMS, w, front), kind)
    sends = 18 * STREAMS + 4 * pieces
    return pl.pallas_call(
        kernel,
        out_shape=jax.ShapeDtypeStruct((1, zrows, columns), F32),
        in_specs=[hbm] * 7 + [pl.BlockSpec(memory_space=pltpu.SMEM)],
        out_specs=local,
        scratch_shapes=[
            vmem((1, bound), jnp.int32),
            pltpu.SMEM((5,), jnp.int32),
            vmem((order, columns), BF16),
            vmem((order, order), BF16),
            vmem((order, bound), BF16),
            vmem((bound, order), BF16),
            vmem((5, front, front), BF16),
            vmem((4, front, front), BF16),
            vmem((bound, front), BF16),
            vmem((front, bound), BF16),
            vmem((order, columns), BF16),
            vmem((order, bound), BF16),
            vmem((bound, front), BF16),
            vmem((STREAMS, 2, 2, 2 * w, front), BF16),
            vmem((STREAMS, 2, 2 * w, front), BF16),
            vmem((pieces, 2, w, front), BF16),
            vmem((pieces, wide, bound), BF16),
            vmem((STREAMS, 2 * w, front), F32),
            vmem((STREAMS, 2 * w, front), BF16),
            vmem((STREAMS, 2 * w, front), BF16),
            vmem((STREAMS, 2 * w, front), BF16),
            level(F32),
            level(BF16),
            level(BF16),
            level(BF16),
            level(F32),
            level(BF16),
            level(BF16),
            level(BF16),
            level(F32),
            level(BF16),
            level(BF16),
            level(BF16),
            level(BF16),
            vmem((STREAMS, 4, 2, w, front), BF16),
            vmem((pieces, 3, zrows, wide), F32),
            vmem((pieces, zrows, wide), BF16),
            vmem((pieces, zrows, wide), BF16),
            vmem((pieces, 2, zrows, wide), BF16),
            vmem((pieces, 2, zrows, wide), BF16),
            pltpu.SemaphoreType.DMA((4 + pieces + 9,)),
            pltpu.SemaphoreType.DMA((sends,)),
            pltpu.SemaphoreType.DMA((sends,)),
        ],
        compiler_params=pltpu.CompilerParams(
            collective_id=0, has_side_effects=True, vmem_limit_bytes=50 * 2**20
        ),
    )(
        *(
            pltpu.with_memory_space_constraint(value, pltpu.HBM)
            for value in (
                leaf_rhs,
                leaf_inverse,
                leaf_coupling,
                leaf_rows,
                front_sizes,
                front_inverse,
                front_coupling,
            )
        ),
        shift_weight,
    )


def solution(mesh):
    in_specs = (
        P("leaf", None, None),
        P("shift", "leaf", None, None),
        P("shift", "leaf", None, None),
        P("leaf", None),
        P(),
        P("shift", None, "leaf", None, None),
        P("shift", None, "leaf", None, None),
        P("shift"),
    )
    out_specs = P("leaf", "shift", None)
    return jax.shard_map(body, mesh=mesh, in_specs=in_specs, out_specs=out_specs, check_vma=False)
```

```python
import jax
import jax.numpy as jnp
from jax import lax
from jax.experimental import pallas as pl
from jax.experimental.pallas import tpu as pltpu
from jax.sharding import PartitionSpec as P

F32 = jnp.float32
BF16 = jnp.bfloat16
NN = (((1,), (0,)), ((), ()))
NT = (((1,), (1,)), ((), ()))
TN = (((0,), (0,)), ((), ()))
STREAMS = 2


def mm(left, right, dims):
    return lax.dot_general(left, right, dims, preferred_element_type=F32)


def kernel(
    rhs_hbm,
    ainv_hbm,
    cpl_hbm,
    rows_hbm,
    sizes_hbm,
    finv_hbm,
    fcpl_hbm,
    weight_ref,
    out_ref,
    rows_ref,
    sizes_ref,
    rhs,
    ainv,
    cpl,
    cpl_t,
    finv,
    fcpl,
    select,
    select_t,
    half,
    lift,
    pick_op,
    hop,
    placed,
    recv0,
    solved1,
    base,
    own1,
    send1,
    recv1,
    solved2,
    own2,
    send2,
    recv2,
    solved3,
    own3,
    send3,
    recv3,
    solved4,
    own4,
    send4,
    recv4,
    back3,
    back3_other,
    back2,
    zown,
    zsend1,
    zrecv1,
    zsend2,
    zrecv2,
    load_sem,
    send_sem,
    recv_sem,
):
    leaf_order, _ = ainv.shape
    front = finv.shape[-1]
    bound = cpl.shape[-1]
    wide = rhs.shape[-1] // (4 * STREAMS)
    w = wide // 2
    zrows = out_ref.shape[1]
    nz = leaf_order // zrows

    p = lax.axis_index("leaf")
    z = lax.axis_index("shift")
    c = lax.rem(p, 2)
    y = lax.rem(p // 2, 4)
    x = p // 8
    h2 = y // 2
    h1 = lax.rem(lax.rem(y, 2) + h2, 2)

    def leaf_of(xx, yy, cc):
        return {"leaf": (xx * 4 + yy) * 2 + cc}

    core_id = leaf_of(x, y, 1 - c)
    y1_id = leaf_of(x, y + 1 - 2 * lax.rem(y, 2), c)
    y3_id = leaf_of(x, 3 - y, c)
    x1_id = leaf_of(x + 1 - 2 * lax.rem(x, 2), y, c)
    x3_id = leaf_of(3 - x, y, c)
    zp_id = {"shift": lax.rem(z + 1, nz)}
    zm_id = {"shift": lax.rem(z + nz - 1, nz)}
    halves = ((1 - h1, 1 - h2), (1 - h1, h2), (h1, 1 - h2), (h1, h2))

    barrier = pltpu.get_barrier_semaphore()
    partners = (core_id, y1_id, y3_id, x1_id, x3_id, zp_id, zm_id)
    for partner in partners:
        pl.semaphore_signal(
            barrier, inc=1, device_id=partner, device_id_type=pl.DeviceIdType.MESH
        )

    def column(s, q):
        a, b = halves[q]
        return pl.multiple_of(((a * 2 + b) * STREAMS + s) * wide, wide)

    loads = {}

    def load(name, src, dst):
        copy = pltpu.make_async_copy(src, dst, load_sem.at[len(loads)])
        loads[name] = copy
        copy.start()

    def load_rhs(s, pair):
        for q in (2 * pair, 2 * pair + 1):
            load(
                ("rhs", s, q),
                rhs_hbm.at[0, :, pl.ds(column(s, q), wide)],
                rhs.at[:, pl.ds((s * 4 + q) * wide, wide)],
            )

    def load_level(level):
        load(("finv", level), finv_hbm.at[0, level, 0], finv.at[level])
        if level < 4:
            load(("fcpl", level), fcpl_hbm.at[0, level, 0], fcpl.at[level])

    load("rows", rows_hbm, rows_ref)
    load("cpl", cpl_hbm.at[0, 0], cpl)
    load("sizes", sizes_hbm, sizes_ref)
    load_rhs(0, 0)
    load("ainv", ainv_hbm.at[0, 0], ainv)
    load_rhs(1, 0)
    load_level(0)

    sent = {}

    def send(name, src, dst, device):
        copy = pltpu.make_async_remote_copy(
            src_ref=src,
            dst_ref=dst,
            send_sem=send_sem.at[len(sent)],
            recv_sem=recv_sem.at[len(sent)],
            device_id=device,
            device_id_type=pl.DeviceIdType.MESH,
        )
        sent[name] = copy
        copy.start()

    def live(value, level):
        lane = lax.broadcasted_iota(jnp.int32, value.shape, len(value.shape) - 1)
        return jnp.where(lane < sizes_ref[level], value, 0.0)

    tiles = range(0, front, 256)

    def solve(operand, level, dst):
        for n in tiles:
            got = mm(operand, finv[level, n : n + 256, :], NT)
            lane = n + lax.broadcasted_iota(jnp.int32, got.shape, 1)
            got = jnp.where(lane < sizes_ref[level], got, 0.0).astype(BF16)
            dst(n, got)

    def into(ref):
        def put(n, got):
            ref[:, n : n + 256] = got

        return put

    def raise_to(solved, level, keep, out):
        for n in tiles:
            got = mm(solved, fcpl[level, :, n : n + 256], NN)
            if keep is not None:
                keep[:, n : n + 256] = got
            if out is not None:
                out[:, n : n + 256] = got.astype(BF16)

    def make_hop(level):
        for n in tiles:
            hop[level - 1, :, n : n + 256] = mm(
                finv[level], fcpl[level, :, n : n + 256], NN
            ).astype(BF16)

    def descend(parent, level, solved, dst):
        for n in tiles:
            got = solved[:, n : n + 256].astype(F32) - mm(
                parent, hop[level - 1, n : n + 256, :], NT
            )
            lane = n + lax.broadcasted_iota(jnp.int32, got.shape, 1)
            got = jnp.where(lane < sizes_ref[level], got, 0.0).astype(BF16)
            dst(n, got)

    loads["rows"].wait()
    for n in tiles:
        row = n + lax.broadcasted_iota(jnp.int32, (256, bound), 0)
        chosen = jnp.where(row == rows_ref[...], 1.0, 0.0)
        select_t[n : n + 256, :] = chosen.astype(BF16)
        select[:, n : n + 256] = jnp.transpose(chosen).astype(BF16)

    loads["cpl"].wait()
    cpl_t[...] = jnp.transpose(cpl[...])

    def halve(s, pair):
        loads["rhs", s, 2 * pair].wait()
        loads["rhs", s, 2 * pair + 1].wait()
        start = (s * 4 + 2 * pair) * wide
        half[:, start : start + 2 * wide] = mm(
            ainv[...], rhs[:, start : start + 2 * wide], NN
        ).astype(BF16)

    def place(s, pair):
        start = (s * 4 + 2 * pair) * wide
        boundary = mm(cpl_t[...], half[:, start : start + 2 * wide], NN)
        boundary_t = jnp.transpose(boundary).astype(BF16)
        for n in tiles:
            got = mm(boundary_t, select_t[n : n + 256, :], NT).astype(BF16)
            for q in range(2):
                for core in range(2):
                    at = (2 * q + core) * w
                    placed[s, pair, core, q * w : q * w + w, n : n + 256] = got[at : at + w]

    def send_place(s, pair):
        send(("place", s, pair), placed.at[s, pair, 1 - c], recv0.at[s, pair], core_id)

    def first(s, pair):
        sent["place", s, pair].wait_recv()
        gathered = placed[s, pair, c].astype(F32) + recv0[s, pair].astype(F32)
        operand = live(gathered, 0).astype(BF16)
        got = []

        def put(n, value):
            got.append(value)
            for q in range(2):
                solved1[s * 4 + 2 * pair + q, c, :, n : n + 256] = value[q * w : q * w + w]

        solve(operand, 0, put)
        level1 = jnp.concatenate(got, axis=1)
        if pair == 0:
            raise_to(level1, 0, None, send1.at[s])
            send_up1(s, 0)
        else:
            raise_to(level1, 0, own1.at[s], None)
        for q in range(2):
            piece = solved1.at[s * 4 + 2 * pair + q, c]
            send(("solved1", s, 2 * pair + q), piece, piece, core_id)

    def send_up1(s, q):
        at = pl.ds(q * w, w)
        send(("up1", s, q), send1.at[s, at], recv1.at[s, at], y1_id)

    def second(s, q):
        sent["up1", s, q].wait_recv()
        at = slice(q * w, q * w + w)
        operand = live(own1[s, at, :] + recv1[s, at, :].astype(F32), 1).astype(BF16)
        solve(operand, 1, into(solved2.at[s, pl.ds(q * w, w)]))
        level2 = solved2[s, at, :]
        if q == 0:
            raise_to(level2, 1, None, send2.at[s])
            send(("up2", s), send2.at[s], recv2.at[s], y3_id)
        else:
            raise_to(level2, 1, own2.at[s], None)

    def third(s):
        sent["up2", s].wait_recv()
        operand = live(own2[s] + recv2[s].astype(F32), 2).astype(BF16)
        solve(operand, 2, into(solved3.at[s]))
        raise_to(solved3[s], 2, own3.at[s], send3.at[s])
        send(("up3", s), send3.at[s], recv3.at[s], x1_id)

    def fourth(s):
        sent["up3", s].wait_recv()
        operand = live(own3[s] + recv3[s].astype(F32), 3).astype(BF16)
        solve(operand, 3, into(solved4.at[s]))
        raise_to(solved4[s], 3, own4.at[s], send4.at[s])
        send(("up4", s), send4.at[s], recv4.at[s], x3_id)

    def turn(s):
        sent["up4", s].wait_recv()
        operand = live(own4[s] + recv4[s].astype(F32), 4).astype(BF16)
        got = []
        solve(operand, 4, lambda n, value: got.append(value))
        back5 = jnp.concatenate(got, axis=1)
        got = []
        descend(back5, 3, solved4.at[s], lambda n, value: got.append(value))
        back4 = jnp.concatenate(got, axis=1)
        descend(back4, 2, solved3.at[s], into(back3.at[s]))
        send(("down2", s), back3.at[s], back3_other.at[s], y3_id)
        descend(back3[s], 1, solved2.at[s, pl.ds(w, w)], into(back2.at[s, 3, c]))
        spread(s, 3)

    def spread(s, q):
        piece = back2.at[s, q, c]
        if q >= 2:
            send(("down1", s, q - 2), piece, back2.at[s, q - 2, c], y1_id)
        send(("core", s, q), piece, piece, core_id)

    def lower(s):
        sent["down2", s].wait_recv()
        descend(back3_other[s], 1, solved2.at[s, pl.ds(0, w)], into(back2.at[s, 2, c]))
        spread(s, 2)

    hz = zrows // 2

    def scatter_first(k, s, q):
        both = back2[s, q].reshape(wide, front)
        picked = base[s * 4 + q].astype(F32) - mm(both, pick_op[...], NT)
        picked = picked.astype(BF16)
        start = (s * 4 + q) * wide

        def rows_of(shift):
            at = pl.multiple_of(lax.rem(z + shift, nz) * zrows, zrows)
            value = half[pl.ds(at, zrows), start : start + wide].astype(F32) - mm(
                lift[pl.ds(at, zrows), :], picked, NT
            )
            return weight_ref[0] * value

        zsend1[k] = rows_of(2).astype(BF16)
        send(("z1p", k), zsend1.at[k, pl.ds(0, hz)], zrecv1.at[k, pl.ds(0, hz)], zp_id)
        send(("z1m", k), zsend1.at[k, pl.ds(hz, hz)], zrecv1.at[k, pl.ds(hz, hz)], zm_id)
        zown[k, 1] = rows_of(1)
        zown[k, 2] = rows_of(3)
        zown[k, 0] = rows_of(0)

    def scatter_second(k):
        sent["z1p", k].wait_recv()
        zsend2[k, 0, :hz] = (zown[k, 1, :hz] + zrecv1[k, :hz].astype(F32)).astype(BF16)
        zsend2[k, 0, hz:] = zown[k, 1, hz:].astype(BF16)
        send(("z2p", k), zsend2.at[k, 0], zrecv2.at[k, 0], zp_id)
        sent["z1m", k].wait_recv()
        zsend2[k, 1, :hz] = zown[k, 2, :hz].astype(BF16)
        zsend2[k, 1, hz:] = (zown[k, 2, hz:] + zrecv1[k, hz:].astype(F32)).astype(BF16)
        send(("z2m", k), zsend2.at[k, 1], zrecv2.at[k, 1], zm_id)

    steps = []

    def relay(s, q):
        sent["down1", s, q].wait_recv()
        send(("core", s, q), back2.at[s, q, c], back2.at[s, q, c], core_id)

    def step(s, q):
        sent["core", s, q].wait_recv()
        k = len(steps)
        steps.append((s, q))
        scatter_first(k, s, q)

    def make_lift():
        lift[...] = mm(ainv[...], cpl[...], NN).astype(BF16)

    def make_pick():
        row = [mm(live(select[...], 0), finv[0, :, n : n + 256], NN).astype(BF16) for n in tiles]
        row = jnp.concatenate(row, axis=1)
        for n in tiles:
            pick_op[:, n : n + 256] = mm(row, fcpl[0, :, n : n + 256], NN).astype(BF16)

    def make_base(s):
        for q in range(4):
            sent["solved1", s, q].wait_recv()
        at = slice(s * 4, s * 4 + 4)
        got = mm(solved1[at].reshape(4 * wide, front), select_t[...], NN).astype(BF16)
        base[at] = got.reshape(4, wide, bound)

    loads["sizes"].wait()
    loads["ainv"].wait()
    halve(0, 0)
    load_rhs(0, 1)
    load_rhs(1, 1)
    place(0, 0)
    for level in range(1, 5):
        load_level(level)
    halve(1, 0)
    place(1, 0)
    pl.semaphore_wait(barrier, len(partners))
    send_place(0, 0)
    send_place(1, 0)
    halve(0, 1)
    loads["finv", 0].wait()
    loads["fcpl", 0].wait()
    first(0, 0)
    send_up1(0, 1)
    first(1, 0)
    send_up1(1, 1)
    place(0, 1)
    send_place(0, 1)
    halve(1, 1)
    first(0, 1)
    loads["finv", 1].wait()
    loads["fcpl", 1].wait()
    second(0, 0)
    place(1, 1)
    send_place(1, 1)
    second(0, 1)
    for level in range(2, 5):
        loads["finv", level].wait()
        if level < 4:
            loads["fcpl", level].wait()
    first(1, 1)
    second(1, 0)
    make_hop(1)
    make_hop(2)
    third(0)
    second(1, 1)
    make_lift()
    third(1)
    make_hop(3)
    fourth(0)
    make_pick()
    make_base(0)
    make_base(1)
    fourth(1)
    turn(0)
    step(0, 3)
    turn(1)
    scatter_second(0)
    lower(0)
    step(1, 3)
    relay(0, 1)
    step(0, 2)
    scatter_second(1)
    lower(1)
    step(0, 1)
    scatter_second(2)
    relay(0, 0)
    relay(1, 1)
    step(1, 2)
    scatter_second(3)
    step(0, 0)
    scatter_second(4)
    relay(1, 0)
    step(1, 1)
    scatter_second(5)
    step(1, 0)
    scatter_second(6)
    scatter_second(7)
    for k, (s, q) in enumerate(steps):
        sent["z2p", k].wait_recv()
        sent["z2m", k].wait_recv()
        out_ref[0, :, pl.ds(column(s, q), wide)] = (
            zown[k, 0] + zrecv2[k, 0].astype(F32) + zrecv2[k, 1].astype(F32)
        )
    for copy in sent.values():
        copy.wait_send()


def body(
    leaf_rhs,
    leaf_inverse,
    leaf_coupling,
    leaf_rows,
    front_sizes,
    front_inverse,
    front_coupling,
    shift_weight,
):
    order = leaf_inverse.shape[-1]
    columns = leaf_rhs.shape[-1]
    front = front_inverse.shape[-1]
    bound = leaf_coupling.shape[-1]
    wide = columns // (4 * STREAMS)
    w = wide // 2
    zrows = order // lax.axis_size("shift")
    pieces = 4 * STREAMS
    vmem = pltpu.VMEM
    hbm = pl.BlockSpec(memory_space=pltpu.HBM)
    local = pl.BlockSpec(memory_space=pltpu.VMEM)
    level = lambda kind: vmem((STREAMS, w, front), kind)
    sends = 18 * STREAMS + 4 * pieces
    return pl.pallas_call(
        kernel,
        out_shape=jax.ShapeDtypeStruct((1, zrows, columns), F32),
        in_specs=[hbm] * 7 + [pl.BlockSpec(memory_space=pltpu.SMEM)],
        out_specs=local,
        scratch_shapes=[
            vmem((1, bound), jnp.int32),
            pltpu.SMEM((5,), jnp.int32),
            vmem((order, columns), BF16),
            vmem((order, order), BF16),
            vmem((order, bound), BF16),
            vmem((bound, order), BF16),
            vmem((5, front, front), BF16),
            vmem((4, front, front), BF16),
            vmem((bound, front), BF16),
            vmem((front, bound), BF16),
            vmem((order, columns), BF16),
            vmem((order, bound), BF16),
            vmem((bound, front), BF16),
            vmem((3, front, front), BF16),
            vmem((STREAMS, 2, 2, 2 * w, front), BF16),
            vmem((STREAMS, 2, 2 * w, front), BF16),
            vmem((pieces, 2, w, front), BF16),
            vmem((pieces, wide, bound), BF16),
            vmem((STREAMS, 2 * w, front), F32),
            vmem((STREAMS, 2 * w, front), BF16),
            vmem((STREAMS, 2 * w, front), BF16),
            vmem((STREAMS, 2 * w, front), BF16),
            level(F32),
            level(BF16),
            level(BF16),
            level(BF16),
            level(F32),
            level(BF16),
            level(BF16),
            level(BF16),
            level(F32),
            level(BF16),
            level(BF16),
            level(BF16),
            level(BF16),
            vmem((STREAMS, 4, 2, w, front), BF16),
            vmem((pieces, 3, zrows, wide), F32),
            vmem((pieces, zrows, wide), BF16),
            vmem((pieces, zrows, wide), BF16),
            vmem((pieces, 2, zrows, wide), BF16),
            vmem((pieces, 2, zrows, wide), BF16),
            pltpu.SemaphoreType.DMA((4 + pieces + 9,)),
            pltpu.SemaphoreType.DMA((sends,)),
            pltpu.SemaphoreType.DMA((sends,)),
        ],
        compiler_params=pltpu.CompilerParams(
            collective_id=0, has_side_effects=True, vmem_limit_bytes=50 * 2**20
        ),
    )(
        *(
            pltpu.with_memory_space_constraint(value, pltpu.HBM)
            for value in (
                leaf_rhs,
                leaf_inverse,
                leaf_coupling,
                leaf_rows,
                front_sizes,
                front_inverse,
                front_coupling,
            )
        ),
        shift_weight,
    )


def solution(mesh):
    in_specs = (
        P("leaf", None, None),
        P("shift", "leaf", None, None),
        P("shift", "leaf", None, None),
        P("leaf", None),
        P(),
        P("shift", None, "leaf", None, None),
        P("shift", None, "leaf", None, None),
        P("shift"),
    )
    out_specs = P("leaf", "shift", None)
    return jax.shard_map(body, mesh=mesh, in_specs=in_specs, out_specs=out_specs, check_vma=False)
```
